128 devices in a mesh: seq: 32 (over x, y, core), tensor: 4 (over z).
Axes of the slice: x: 4, y: 4, z: 4, core: 2. Of those that a mesh axis runs over, the one named last changes fastest.
Arguments:
- inputs: bfloat16 [131072, 2048], P('seq', 'tensor'), may hold values from -6 to 6
- out_grad: bfloat16 [131072, 2048], P('seq', 'tensor'), may hold values from -6 to 6
- router_score: float32 [131072], P('seq'), may hold values from 0.1 to 1
- route_index: int32 [32, 512], P('seq'), may hold values from 0 to 4095, as said below
- block_count: int32 [32], P('seq'), may hold values from 1 to 4, 64 in all
- w_in: bfloat16 [2048, 8192], P('seq', 'tensor'), may hold values from -0.125 to 0.125
- w_out: bfloat16 [8192, 2048], P('tensor', 'seq'), may hold values from -0.0625 to 0.0625
Outputs:
- input_grad: bfloat16 [131072, 2048], P('seq', 'tensor')
- score_grad: float32 [131072], P('seq')
The draws below stay inside these ranges and needn't reach their ends.
Inputs may be any that keep to these rules, and one draw needn't show every extreme that they name: `route_index`: row j holds 512 distinct positions within shard j; its first block_count[j] * 128 entries are the routed tokens, the rest padding. `block_count`: the counts sum to exactly 64.
All inputs are finite; a program needn't handle non-finite values.
Results may differ from the reference program's by a relative error of at most 0.012.
Values may be sent and summed in bfloat16 or wider, within the bound.
No kernel may reach another device: no remote copies, remote signals or barrier semaphores. Data moves between devices by JAX's collectives and lax.ppermute only.
A program may use at most 128 MiB of HBM per device.

```python
import math
import jax
import jax.numpy as jnp
import numpy as np
from jax import lax

D = 2048
FF = 8192
TOK_DEV = 4096
BLK = 128
SHARDS = 32
TOKENS = 131072
AVG_BLOCKS = 2
CAP_BLOCKS = 4


def draw_route_index(key, part):
    shard_keys = jax.random.split(key, SHARDS)

    def one_shard(shard_key):
        return jax.random.permutation(shard_key, TOK_DEV)[:CAP_BLOCKS * BLK].astype(jnp.int32)
    return jax.vmap(one_shard)(shard_keys)


def shard_levels(rng, dims, cuts, smallest, top_value):
    def one(axis_at, blocks):
        steps = jax.random.uniform(jax.random.fold_in(jax.random.fold_in(rng, 6), axis_at), (blocks,), jnp.float32, smallest / len(cuts), top_value / len(cuts))
        return jnp.repeat(jnp.exp(steps), dims[axis_at] // blocks).reshape((-1,) + (1,) * (len(dims) - axis_at - 1))

    loudness = one(*cuts[0])
    for cut in cuts[1:]:
        loudness = loudness * one(*cut)
    return loudness


def length_profile(number_of, total, limit, skew):
    loads = [(1 << 20) // math.isqrt(standing ** skew) + 1 for standing in range(2, number_of + 1)]
    rest, holding = total - limit - (number_of - 1), [1] * (number_of - 1)
    while rest > 0:
        free = [i for i in range(number_of - 1) if holding[i] < limit]
        whole, remaining = sum([loads[i] for i in free]), rest
        for i in free:
            more = min(limit - holding[i], max(1, remaining * loads[i] // whole), rest)
            holding[i] = holding[i] + more
            rest = rest - more
    return np.array([limit] + holding)


def ragged_sizes(key, number_of, total, reach, skew):
    if number_of == 2:
        one = jax.random.randint(key, (), max(1, total - reach), min(reach, total - 1) + 1)
        return jnp.stack([one, total - one])
    sizes = jnp.asarray(length_profile(number_of, total, reach, skew), jnp.int32)
    couples = (number_of - 1) // 2
    giver, sink = sizes[1:1 + 2 * couples:2], sizes[2:2 + 2 * couples:2]
    room = jnp.minimum(giver - 1, reach - sink)
    passed = jax.random.randint(jax.random.fold_in(key, 1), (couples,), 0, 1 << 20) % (room + 1)
    sizes = sizes.at[1:1 + 2 * couples:2].set(giver - passed).at[2:2 + 2 * couples:2].set(sink + passed)
    return sizes[jax.random.permutation(jax.random.fold_in(key, 2), number_of)]


def gaussian(stream_key, extent, width, reach, cuts=(), kind=jnp.bfloat16):
    result = jax.random.normal(stream_key, extent, jnp.float32) * width
    if len(cuts) > 0:
        result = shard_levels(stream_key, extent, cuts, -0.22, 0.18) * result
    return jnp.clip(result, min=-reach, max=reach).astype(kind)


def setup_inputs(seed: int = 0) -> dict:
    key_of = jax.random.split(jax.random.key(seed), 8)
    return {
        "inputs": gaussian(key_of[0], (TOKENS, D), 1.0, 6.0, ((0, 32), (1, 4))),
        "out_grad": gaussian(key_of[1], (TOKENS, D), 1.0, 6.0, ((0, 32), (1, 4))),
        "router_score": jnp.clip(0.1 + 0.9 * jax.random.uniform(key_of[2], (TOKENS,), jnp.float32) ** shard_levels(key_of[2], (TOKENS,), ((0, 32),), -0.2, 0.2), 0.1, 1.0),
        "route_index": draw_route_index(jax.random.fold_in(key_of[7], 71), 0),
        "block_count": ragged_sizes(key_of[4], SHARDS, SHARDS * AVG_BLOCKS, CAP_BLOCKS, 2).astype(jnp.int32),
        "w_in": gaussian(key_of[5], (D, FF), D ** -0.5, 0.125, ((0, 32), (1, 4))),
        "w_out": gaussian(key_of[6], (FF, D), FF ** -0.5, 0.0625, ((0, 4), (1, 32))),
    }


gelu_coeff = 0.7978845608028654
cubic_coeff = 0.044715


def gelu_pair(values):
    inner = gelu_coeff * (values + cubic_coeff * values * values * values)
    tangent = jnp.tanh(inner)
    forward = 0.5 * values * (1.0 + tangent)
    slope = 0.5 * (1.0 + tangent) + 0.5 * values * (1.0 - tangent * tangent) * gelu_coeff * (1.0 + 3.0 * cubic_coeff * values * values)
    return forward, slope


def round_keep(values):
    narrow = lax.optimization_barrier(values.astype(jnp.bfloat16))
    return narrow.astype(jnp.float32)


def reference(inputs, out_grad, router_score, route_index, block_count, w_in, w_out):
    route_rows = CAP_BLOCKS * BLK
    live_total = SHARDS * AVG_BLOCKS * BLK
    step_rows = AVG_BLOCKS * BLK
    counts = block_count.astype(jnp.int32)
    offsets = (jnp.cumsum(counts) - counts).astype(jnp.int32)
    slot_ids = jnp.arange(route_rows, dtype=jnp.int32)
    target = offsets[:, None] * BLK + slot_ids[None, :]
    is_live = slot_ids[None, :] < (counts * BLK)[:, None]
    target = jnp.where(is_live, target, live_total).astype(jnp.int32)
    shard_ids = jnp.arange(SHARDS, dtype=jnp.int32)
    source = (shard_ids[:, None] * TOK_DEV + route_index).astype(jnp.int32)
    gathered = jnp.zeros((live_total,), jnp.int32).at[target.reshape(-1)].set(source.reshape(-1), mode="drop")
    weight_in = w_in.astype(jnp.float32)
    weight_out = w_out.astype(jnp.float32)

    def one_step(picked):
        chosen = inputs[picked].astype(jnp.float32)
        grads = out_grad[picked].astype(jnp.float32)
        scores = router_score[picked].astype(jnp.float32)
        hidden = jnp.dot(chosen, weight_in)
        forward, slope = gelu_pair(hidden)
        active = round_keep(forward)
        upstream = jnp.dot(grads, weight_out.T)
        score_part = jnp.sum(upstream * active, axis=1)
        hidden_grad = round_keep(scores[:, None] * upstream * slope)
        input_part = jnp.dot(hidden_grad, weight_in.T).astype(jnp.bfloat16)
        return input_part, score_part

    input_rows, score_rows = lax.map(one_step, gathered.reshape(-1, step_rows))
    input_grad = jnp.zeros((TOKENS, D), jnp.bfloat16).at[gathered].set(input_rows.reshape(-1, D))
    score_grad = jnp.zeros((TOKENS,), jnp.float32).at[gathered].set(score_rows.reshape(-1).astype(jnp.float32))
    return input_grad, score_grad
```

```python
import functools

import jax
import jax.numpy as jnp
from jax import lax
from jax.experimental import pallas as pl
from jax.experimental.pallas import tpu as pltpu
from jax.sharding import PartitionSpec as P

BLK = 128
SIDE = 4
CHIPS = SIDE * SIDE

gelu_coeff = 0.7978845608028654
cubic_coeff = 0.044715

RELS = (0, -1, 1, 2)


def gelu_pair(values):
    inner = gelu_coeff * (values + cubic_coeff * values * values * values)
    tangent = jnp.tanh(inner)
    forward = 0.5 * values * (1.0 + tangent)
    slope = 0.5 * (1.0 + tangent) + 0.5 * values * (1.0 - tangent * tangent) * gelu_coeff * (
        1.0 + 3.0 * cubic_coeff * values * values
    )
    return (forward, slope)


def seq_pairs(target):
    pairs = []
    for x in range(SIDE):
        for y in range(SIDE):
            for c in range(2):
                tx, ty, tc = target(x, y, c)
                pairs.append((((x * SIDE) + y) * 2 + c, ((tx % SIDE) * SIDE + ty % SIDE) * 2 + tc))
    return pairs


def ring(step, phase):
    return seq_pairs(lambda x, y, c: (x + step, y, c) if (c == phase) else (x, y + step, c))


SWAP = seq_pairs(lambda x, y, c: (x, y, 1 - c))


def swap(value):
    return lax.ppermute(value, "seq", SWAP)


def hop(value, step, phase):
    return lax.ppermute(value, "seq", ring(step, phase))


def zhop(value, step):
    return lax.ppermute(value, "tensor", [(i, (i + step) % SIDE) for i in range(SIDE)])


TILE = 256
DOT = functools.partial(
    lax.dot_general, preferred_element_type=jnp.float32
)
NN = (((1,), (0,)), ((), ()))
NT = (((1,), (1,)), ((), ()))


def tile_state(meta, step):
    own = step < 2
    count = jnp.where(own, meta[48], meta[49])
    start = jnp.where(own, step, step - 2) * (TILE // BLK)
    return own, start < count


def columns(rows_ref, meta, first):
    parts = []
    for k in range(first, first + SIDE):
        parts.append(rows_ref[meta[k], :, pl.ds(pl.multiple_of(meta[16 + k] * BLK, BLK), BLK)])
    return jnp.concatenate(parts, axis=1)


def partial_kernel(groups, meta, xo, xp, go, gp, *refs):
    w_ins, w_outs = refs[:groups], refs[groups : 2 * groups]
    hid, up = refs[2 * groups :]
    step = pl.program_id(0)
    own, live = tile_state(meta, step)

    def work(x_ref, g_ref):
        for rows, weights, total in ((x_ref, w_ins, hid), (g_ref, w_outs, up)):
            acc = None
            for j in range(groups):
                term = DOT(columns(rows, meta, SIDE * j), weights[j][...], NN)
                acc = term if acc is None else acc + term
            total[...] = acc

    @pl.when(jnp.logical_and(live, own))
    def _():
        work(xo, go)

    @pl.when(jnp.logical_and(live, jnp.logical_not(own)))
    def _():
        work(xp, gp)


def row_specs():
    own = pl.BlockSpec((SIDE, TILE, 512), lambda m, meta: (0, jnp.minimum(m, 1), 0))
    par = pl.BlockSpec((SIDE, TILE, 512), lambda m, meta: (0, jnp.maximum(m - 2, 0), 0))
    return own, par


def whole(shape):
    return pl.BlockSpec(shape, lambda m, meta: (0,) * len(shape), pipeline_mode=pl.Buffered(1))


def partial_sums(meta, xo, xp, go, gp, w_ins, w_outs):
    groups = len(w_ins)
    own, par = row_specs()
    tile = pl.BlockSpec((TILE, 1024), lambda m, meta: (m, 0))
    return pl.pallas_call(
        functools.partial(partial_kernel, groups),
        grid_spec=pltpu.PrefetchScalarGridSpec(
            num_scalar_prefetch=1,
            grid=(4,),
            in_specs=[own, par, own, par] + [whole((512, 1024))] * (2 * groups),
            out_specs=[tile, tile],
        ),
        out_shape=[jax.ShapeDtypeStruct((1024, 1024), jnp.float32)] * 2,
        compiler_params=pltpu.CompilerParams(vmem_limit_bytes=40 << 20),
        name="partial_sums",
    )(meta, xo, xp, go, gp, *w_ins, *w_outs)


def hidden_kernel(meta, hid, up, xo, xp, go, gp, so, sp, wi3, wo3, g0, g1, g2, g3, hg, score, oo, op, wabs, wv, sems, osem):
    step = pl.program_id(0)
    own, live = tile_state(meta, step)
    groups = (g0, g1, g2, g3)

    def piece_copy(k):
        return pltpu.make_async_copy(
            groups[k // SIDE].at[pl.ds((k % SIDE) * BLK, BLK)], wv.at[meta[32 + k]], sems.at[k]
        )

    @pl.when(step == 0)
    def _():
        for k in range(CHIPS):
            piece_copy(k).start()

    def work(x_ref, g_ref, s_ref):
        hidden = hid[...] + DOT(columns(x_ref, meta, 12), wi3[...], NN)
        upstream = up[...] + DOT(columns(g_ref, meta, 12), wo3[...], NN)
        forward, slope = gelu_pair(hidden)
        active = forward.astype(jnp.bfloat16).astype(jnp.float32)
        score[...] = jnp.sum(upstream * active, axis=1, keepdims=True)
        hg[...] = (s_ref[...] * upstream * slope).astype(jnp.bfloat16)

    @pl.when(jnp.logical_and(live, own))
    def _():
        work(xo, go, so)

    @pl.when(jnp.logical_and(live, jnp.logical_not(own)))
    def _():
        work(xp, gp, sp)

    @pl.when(step == 0)
    def _():
        for k in range(CHIPS):
            piece_copy(k).wait()
        pltpu.make_async_copy(wv, wabs, osem).start()

    def finish(out):
        quarter = wv[pl.ds(meta[50] * SIDE, SIDE)].reshape(512, 1024)
        out[...] = DOT(hg[...], quarter, NT).astype(jnp.bfloat16)

    @pl.when(jnp.logical_and(live, own))
    def _():
        finish(oo)

    @pl.when(jnp.logical_and(live, jnp.logical_not(own)))
    def _():
        finish(op)

    @pl.when(step == 3)
    def _():
        pltpu.make_async_copy(wv, wabs, osem).wait()


def own_out():
    return pl.BlockSpec((TILE, 512), lambda m, meta: (jnp.minimum(m, 1), 0))


def par_out():
    return pl.BlockSpec((TILE, 512), lambda m, meta: (jnp.maximum(m - 2, 0), 0))


def hidden_stage(meta, hid, up, xo, xp, go, gp, so, sp, w_in_groups, wo3):
    own, par = row_specs()
    tile = pl.BlockSpec((TILE, 1024), lambda m, meta: (m, 0))
    col_own = pl.BlockSpec((TILE, 1), lambda m, meta: (jnp.minimum(m, 1), 0))
    col_par = pl.BlockSpec((TILE, 1), lambda m, meta: (jnp.maximum(m - 2, 0), 0))
    col = pl.BlockSpec((TILE, 1), lambda m, meta: (m, 0))
    anywhere = pl.BlockSpec(memory_space=pl.ANY)
    part = jax.ShapeDtypeStruct((512, 512), jnp.bfloat16)
    return pl.pallas_call(
        hidden_kernel,
        grid_spec=pltpu.PrefetchScalarGridSpec(
            num_scalar_prefetch=1,
            grid=(4,),
            in_specs=[tile, tile, own, par, own, par, col_own, col_par]
            + [whole((512, 1024))] * 2
            + [anywhere] * 4,
            out_specs=[tile, col, own_out(), par_out(), anywhere],
            scratch_shapes=[
                pltpu.VMEM((CHIPS, BLK, 1024), jnp.bfloat16),
                pltpu.SemaphoreType.DMA((CHIPS,)),
                pltpu.SemaphoreType.DMA,
            ],
        ),
        out_shape=[
            jax.ShapeDtypeStruct((1024, 1024), jnp.bfloat16),
            jax.ShapeDtypeStruct((1024, 1), jnp.float32),
            part,
            part,
            jax.ShapeDtypeStruct((CHIPS, BLK, 1024), jnp.bfloat16),
        ],
        compiler_params=pltpu.CompilerParams(vmem_limit_bytes=40 << 20),
        name="hidden_stage",
    )(meta, hid, up, xo, xp, go, gp, so, sp, w_in_groups[3], wo3, *w_in_groups)


def output_kernel(meta, hg, wabs, a_own, a_par, b_own, b_par, c_own, c_par):
    step = pl.program_id(0)
    own, live = tile_state(meta, step)

    def finish(outs):
        for k, out in enumerate(outs):
            quarter = wabs[pl.ds(meta[51 + k] * SIDE, SIDE)].reshape(512, 1024)
            out[...] = DOT(hg[...], quarter, NT).astype(jnp.bfloat16)

    @pl.when(jnp.logical_and(live, own))
    def _():
        finish((a_own, b_own, c_own))

    @pl.when(jnp.logical_and(live, jnp.logical_not(own)))
    def _():
        finish((a_par, b_par, c_par))


def output_stage(meta, hg, wabs):
    part = jax.ShapeDtypeStruct((512, 512), jnp.bfloat16)
    return pl.pallas_call(
        output_kernel,
        grid_spec=pltpu.PrefetchScalarGridSpec(
            num_scalar_prefetch=1,
            grid=(4,),
            in_specs=[
                pl.BlockSpec((TILE, 1024), lambda m, meta: (m, 0)),
                whole((CHIPS, BLK, 1024)),
            ],
            out_specs=[own_out(), par_out()] * 3,
        ),
        out_shape=[part] * 6,
        compiler_params=pltpu.CompilerParams(vmem_limit_bytes=40 << 20),
        name="output_stage",
    )(meta, hg, wabs)


def per_device(inputs, out_grad, router_score, route_index, block_count, w_in, w_out):
    route_rows = route_index.shape[1]
    picked = route_index[0]
    own_count = block_count[0]
    seq = lax.axis_index("seq")
    z = lax.axis_index("tensor")
    c = seq % 2
    y = (seq // 2) % SIDE
    x = seq // (2 * SIDE)

    w_out_t = w_out.T
    half = w_in.shape[1] // 2

    def cut(w, which):
        return lax.dynamic_slice_in_dim(w, which * half, half, axis=1)

    sent = jnp.stack([cut(w_in, 1 - c), cut(w_out_t, 1 - c)])
    got = swap(sent)

    def joined(w, other):
        mine = cut(w, c)
        return jnp.where(
            c == 0, jnp.concatenate([mine, other], 0), jnp.concatenate([other, mine], 0)
        )

    s_in, s_out = joined(w_in, got[0]), joined(w_out_t, got[1])

    def gather4(a, b, phase):
        a_f, b_b = hop(a, 1, phase), hop(b, -1, phase)
        a_b, b_f = hop(a, -1, phase), hop(b, 1, phase)
        a_2, b_2 = hop(a_f, 1, phase), hop(b_b, -1, phase)
        return [a, a_f, a_b, a_2], [b, b_f, b_b, b_2]

    in_pieces, out_pieces = gather4(s_in, s_out, 0)
    group_in, group_out = jnp.concatenate(in_pieces, 0), jnp.concatenate(out_pieces, 0)
    w_ins, w_outs = gather4(group_in, group_out, 1)

    def rows_of(a):
        return a.at[picked].get(mode="promise_in_bounds", unique_indices=True)

    xs, gs = rows_of(inputs), rows_of(out_grad)
    x_f, g_b = zhop(xs, 1), zhop(gs, -1)
    x_b, g_f = zhop(xs, -1), zhop(gs, 1)
    x_2, g_2 = zhop(x_f, 1), zhop(g_b, -1)
    xo, go = jnp.stack([xs, x_f, x_b, x_2]), jnp.stack([gs, g_f, g_b, g_2])
    xp, gp = swap(xo), swap(go)

    side = jnp.concatenate(
        [rows_of(router_score), jnp.full((BLK,), own_count.astype(jnp.float32))]
    )
    side_p = swap(side)
    so, sp = side[:route_rows, None], side_p[:route_rows, None]
    par_count = side_p[route_rows].astype(jnp.int32)

    first = jnp.array(RELS, jnp.int32)[None, :]
    second = jnp.array(RELS, jnp.int32)[:, None]
    zero = jnp.zeros((SIDE, SIDE), jnp.int32)
    px = (x + jnp.where(c == 0, first + zero, second + zero)) % SIDE
    py = (y + jnp.where(c == 0, second + zero, first + zero)) % SIDE
    rel = (px - z) % SIDE
    slot = jnp.where(rel == 0, 0, jnp.where(rel == 3, 1, jnp.where(rel == 1, 2, 3)))
    tail = jnp.stack(
        [own_count, par_count, (z + 2) % SIDE, (z + 1) % SIDE, (z + 3) % SIDE, z]
    ).astype(jnp.int32)
    meta = jnp.concatenate(
        [slot.reshape(-1), py.reshape(-1), (px * SIDE + py).reshape(-1), tail]
    ).astype(jnp.int32)

    hid, up = partial_sums(meta, xo, xp, go, gp, w_ins[:3], w_outs[:3])
    hg, score, o2_own, o2_par, wabs = hidden_stage(
        meta, hid, up, xo, xp, go, gp, so, sp, w_ins, w_outs[3]
    )
    f1_own, f1_par, b1_own, b1_par, o0_own, o0_par = output_stage(meta, hg, wabs)

    def both(own, par):
        return own.astype(jnp.float32) + swap(par).astype(jnp.float32)

    row_scores = score[:route_rows, 0] + swap(score[route_rows:, 0])
    row_scores = row_scores + zhop(row_scores, 2)
    row_scores = row_scores + zhop(row_scores, 1)

    mid = route_rows // 2
    r2 = both(o2_own, o2_par).astype(jnp.bfloat16)
    through_f, through_b = zhop(r2[:mid], 1), zhop(r2[mid:], -1)
    r_f, r_b = both(f1_own, f1_par), both(b1_own, b1_par)
    low_b = zhop(r_f[mid:].astype(jnp.bfloat16), 1)
    low_a = zhop(r_b[:mid].astype(jnp.bfloat16), -1)
    full_a = zhop((r_f[:mid] + through_f.astype(jnp.float32)).astype(jnp.bfloat16), 1)
    full_b = zhop((r_b[mid:] + through_b.astype(jnp.float32)).astype(jnp.bfloat16), -1)
    r0 = both(o0_own, o0_par)
    top = r0[:mid] + full_a.astype(jnp.float32) + low_a.astype(jnp.float32)
    bottom = r0[mid:] + full_b.astype(jnp.float32) + low_b.astype(jnp.float32)
    mine_grads = jnp.concatenate([top, bottom], 0).astype(jnp.bfloat16)

    is_mine = jnp.arange(route_rows, dtype=jnp.int32) < own_count * BLK
    mine_grads = jnp.where(is_mine[:, None], mine_grads, jnp.zeros((), jnp.bfloat16))
    mine_scores = jnp.where(is_mine, row_scores, 0.0)
    settings = dict(mode="promise_in_bounds", unique_indices=True)
    input_grad = jnp.zeros(inputs.shape, jnp.bfloat16).at[picked].set(mine_grads, **settings)
    score_grad = jnp.zeros(router_score.shape, jnp.float32).at[picked].set(mine_scores, **settings)
    return (input_grad, score_grad)


def solution(mesh):
    placed = (
        P("seq", "tensor"),
        P("seq", "tensor"),
        P("seq"),
        P("seq", None),
        P("seq"),
        P("seq", "tensor"),
        P("tensor", "seq"),
    )
    return jax.shard_map(
        per_device,
        mesh=mesh,
        in_specs=placed,
        out_specs=(P("seq", "tensor"), P("seq")),
        check_vma=False,
    )
```

```python
import functools

import jax
import jax.numpy as jnp
from jax import lax
from jax.experimental import pallas as pl
from jax.experimental.pallas import tpu as pltpu
from jax.sharding import PartitionSpec as P


BLK = 128
SIDE = 4
CHIPS = SIDE * SIDE

gelu_coeff = 0.7978845608028654
cubic_coeff = 0.044715

RELS = (0, -1, 1, 2)


def gelu_pair(values):
    square = values * values
    inner = values * (gelu_coeff + gelu_coeff * cubic_coeff * square)
    h = 0.5 * jnp.tanh(inner) + 0.5
    forward = values * h
    bend = values * (2.0 * gelu_coeff + 6.0 * gelu_coeff * cubic_coeff * square)
    slope = h + h * ((1.0 - h) * bend)
    return (forward, slope)


def seq_pairs(target):
    pairs = []
    for x in range(SIDE):
        for y in range(SIDE):
            for c in range(2):
                tx, ty, tc = target(x, y, c)
                pairs.append((((x * SIDE) + y) * 2 + c, ((tx % SIDE) * SIDE + ty % SIDE) * 2 + tc))
    return pairs


def ring(step, phase):
    return seq_pairs(lambda x, y, c: (x + step, y, c) if (c == phase) else (x, y + step, c))


SWAP = seq_pairs(lambda x, y, c: (x, y, 1 - c))


def swap(value):
    return lax.ppermute(value, "seq", SWAP)


def hop(value, step, phase):
    return lax.ppermute(value, "seq", ring(step, phase))


ZPAIRS = []
for z_at in range(SIDE):
    for s_at in range(2 * CHIPS):
        to = (z_at + (1 if s_at % 2 == 0 else -1)) % SIDE
        ZPAIRS.append((s_at * SIDE + z_at, s_at * SIDE + to))


def zdir(value):
    return lax.ppermute(value, ("seq", "tensor"), ZPAIRS)


def zhop(value, step):
    return lax.ppermute(value, "tensor", [(i, (i + step) % SIDE) for i in range(SIDE)])


TILE = 256
ROWS = 512
TOK = 4096
SPAN = 1024
DOT = functools.partial(lax.dot_general, preferred_element_type=jnp.float32)
NN = (((1,), (0,)), ((), ()))
NT = (((1,), (1,)), ((), ()))
ANY = pl.BlockSpec(memory_space=pl.ANY)
HBM = pl.BlockSpec(memory_space=pltpu.MemorySpace.HBM)


def params(mib):
    return pltpu.CompilerParams(vmem_limit_bytes=mib << 20)


def whole(shape):
    return pl.BlockSpec(shape, lambda m, meta: (0,) * len(shape))


def pick_kernel(count, idx_hbm, score_hbm, x_hbm, g_hbm, out, s_out, idx, score, xv, gv, hot, sems):
    small = [
        pltpu.make_async_copy(idx_hbm, idx, sems.at[2]),
        pltpu.make_async_copy(score_hbm, score, sems.at[3]),
    ]
    copies = [
        pltpu.make_async_copy(x_hbm, xv, sems.at[0]),
        pltpu.make_async_copy(g_hbm, gv, sems.at[1]),
    ]
    for copy in small + copies:
        copy.start()
    for copy in small:
        copy.wait()
    column = jnp.broadcast_to(idx[...], (BLK, ROWS)).T
    for r in range(ROWS // BLK):

        @pl.when(r < count[0])
        def _(r=r):
            at = jnp.broadcast_to(column[r * BLK : (r + 1) * BLK, :1], (BLK, TOK))
            same = lax.broadcasted_iota(jnp.int32, (BLK, TOK), 1) == at
            hot[r * BLK : (r + 1) * BLK, :] = jnp.where(same, 1.0, 0.0).astype(jnp.bfloat16)
            s_out[r * BLK : (r + 1) * BLK, :] = jnp.sum(
                jnp.where(same, score[...], 0.0), axis=1, keepdims=True
            )

    for k, (copy, rows) in enumerate(zip(copies, (xv, gv))):
        copy.wait()

        @pl.when(count[0] <= 2)
        def _(k=k, rows=rows):
            at = pl.ds(0, TILE)
            out[k, at, :] = DOT(hot[at, :], rows[...], NN).astype(jnp.bfloat16)

        @pl.when(count[0] > 2)
        def _(k=k, rows=rows):
            out[k] = DOT(hot[...], rows[...], NN).astype(jnp.bfloat16)


def pick(count, idx, score, inputs, out_grad):
    return pl.pallas_call(
        pick_kernel,
        grid_spec=pltpu.PrefetchScalarGridSpec(
            num_scalar_prefetch=1,
            grid=(1,),
            in_specs=[HBM] * 4,
            out_specs=[whole((2, ROWS, 512)), whole((ROWS, 1))],
            scratch_shapes=[
                pltpu.VMEM((1, ROWS), jnp.int32),
                pltpu.VMEM((1, TOK), jnp.float32),
                pltpu.VMEM((TOK, 512), jnp.bfloat16),
                pltpu.VMEM((TOK, 512), jnp.bfloat16),
                pltpu.VMEM((ROWS, TOK), jnp.bfloat16),
                pltpu.SemaphoreType.DMA((4,)),
            ],
        ),
        out_shape=[
            jax.ShapeDtypeStruct((2, ROWS, 512), jnp.bfloat16),
            jax.ShapeDtypeStruct((ROWS, 1), jnp.float32),
        ],
        compiler_params=params(62),
        name="pick",
    )(count, idx, score, inputs, out_grad)


def tile_live(meta, half, tile):
    return tile * (TILE // BLK) < meta[48 + half]


def half_kernel(half, meta, *refs):
    rows, scale_ref = refs[:4], refs[4]
    (sw, p_f, p_b, h_in, h_out, y0f, y0b, yrf, yrb, yhf, yhb) = refs[5:16]
    last = (refs[16:19], refs[19:22])
    out, out_0, score, rv, wi, wo, hg, row_sems, sems = refs[22:]
    tile = pl.program_id(0)
    row_copies = [
        pltpu.make_async_copy(rows[r], rv.at[:, meta[54 + r]], row_sems.at[r]) for r in range(4)
    ]
    groups = [[], [], [], []]
    for w, target in ((0, wi), (1, wo)):
        line = [sw.at[w], p_f.at[w], p_b.at[w], (h_in, h_out)[w]]
        for y0, yr, yh in ((y0f, yrf, yhf), (y0b, yrb, yhb)):
            line += [y0.at[w], yr.at[pl.ds(2 * w, 2)], None, yh.at[w]]
        line += [last[w][0], last[w][1], None, last[w][2]]
        for k in range(CHIPS):
            if line[k] is not None:
                to = target.at[pl.ds(k, 2)] if k % 4 == 1 and k > 4 else target.at[k]
                groups[k // 4].append(pltpu.make_async_copy(line[k], to, sems.at[w, k]))

    @pl.when(tile == 0)
    def _():
        for copy in row_copies + groups[0] + groups[1] + groups[2] + groups[3]:
            copy.start()
        for copy in row_copies + groups[0] + groups[1]:
            copy.wait()

    at = pl.ds(pl.multiple_of(tile * TILE, TILE), TILE)

    def columns(which, first, last):
        parts = []
        for k in range(first, last):
            lanes = pl.ds(pl.multiple_of(meta[16 + k] * BLK, BLK), BLK)
            parts.append(rv[which, meta[k], at, lanes])
        return jnp.concatenate(parts, axis=1)

    live = tile_live(meta, half, tile)

    @pl.when(tile == 0)
    def _():
        for copy in groups[2] + groups[3]:
            copy.wait()

    @pl.when(live)
    def _():
        xs, gs, scale = columns(0, 0, CHIPS), columns(1, 0, CHIPS), scale_ref[...]
        total = None
        for n in range(4):
            cols = pl.ds(n * 256, 256)
            hidden = DOT(xs, wi[:, :, cols].reshape(CHIPS * BLK, 256), NN)
            upstream = DOT(gs, wo[:, :, cols].reshape(CHIPS * BLK, 256), NN)
            forward, slope = gelu_pair(hidden)
            active = forward.astype(jnp.bfloat16).astype(jnp.float32)
            term = jnp.sum(upstream * active, axis=1, keepdims=True)
            total = term if total is None else total + term
            hg[:, cols] = (scale * upstream * slope).astype(jnp.bfloat16)
        score[...] = total
        for q in range(4):
            where = meta[50 + q] * SIDE
            quarter = jnp.concatenate([wi[meta[32 + where + b]] for b in range(SIDE)], axis=0)
            result = DOT(hg[...], quarter, NT).astype(jnp.bfloat16)
            if q < 3:
                out[q] = result
            else:
                out_0[...] = result


def half_stage(half, meta, rows, s, pieces):
    col = pl.BlockSpec((TILE, 1), lambda m, meta: (m, 0))
    return pl.pallas_call(
        functools.partial(half_kernel, half),
        grid_spec=pltpu.PrefetchScalarGridSpec(
            num_scalar_prefetch=1,
            grid=(2,),
            in_specs=[ANY] * 4 + [col] + [ANY] * 17,
            out_specs=[
                pl.BlockSpec((3, TILE, 512), lambda m, meta: (0, m, 0)),
                pl.BlockSpec((TILE, 512), lambda m, meta: (m, 0)),
                col,
            ],
            scratch_shapes=[
                pltpu.VMEM((2, SIDE, ROWS, 512), jnp.bfloat16),
                pltpu.VMEM((CHIPS, BLK, 1024), jnp.bfloat16),
                pltpu.VMEM((CHIPS, BLK, 1024), jnp.bfloat16),
                pltpu.VMEM((TILE, 1024), jnp.bfloat16),
                pltpu.SemaphoreType.DMA((4,)),
                pltpu.SemaphoreType.DMA((2, CHIPS)),
            ],
        ),
        out_shape=[
            jax.ShapeDtypeStruct((3, ROWS, 512), jnp.bfloat16),
            jax.ShapeDtypeStruct((ROWS, 512), jnp.bfloat16),
            jax.ShapeDtypeStruct((ROWS, 1), jnp.float32),
        ],
        compiler_params=params(62),
        name="half_stage",
    )(meta, *rows, s, *pieces)


def marks_kernel(idx, out):
    token = lax.broadcasted_iota(jnp.int32, (SPAN, ROWS), 0) + pl.program_id(0) * SPAN
    hot = jnp.where(token == jnp.broadcast_to(idx[...], (SPAN, ROWS)), 1.0, 0.0)
    out[...] = hot.astype(jnp.bfloat16)


def marks(idx):
    return pl.pallas_call(
        marks_kernel,
        grid=(TOK // SPAN,),
        in_specs=[pl.BlockSpec((1, ROWS), lambda m: (0, 0))],
        out_specs=pl.BlockSpec((SPAN, ROWS), lambda m: (m, 0)),
        out_shape=jax.ShapeDtypeStruct((TOK, ROWS), jnp.bfloat16),
        compiler_params=params(62),
        name="marks",
    )(idx)


def place_kernel(count, hot, own, other, full_a, full_b, low_a, low_b, out, rows):
    step = pl.program_id(0)
    mid = ROWS // 2

    @pl.when(step == 0)
    def _():
        for at, parts in ((0, (full_a, low_a)), (mid, (full_b, low_b))):
            here = pl.ds(at, mid)
            total = own[here, :].astype(jnp.float32) + other[here, :].astype(jnp.float32)
            for part in parts:
                total = total + part[...].astype(jnp.float32)
            at_row = lax.broadcasted_iota(jnp.int32, (mid, 512), 0) + at
            total = jnp.where(at_row < count[0] * BLK, total, 0.0)
            rows[here, :] = total.astype(jnp.bfloat16)

    out[...] = DOT(hot[...], rows[...], NN).astype(jnp.bfloat16)


def place(count, hot, own, other, full_a, full_b, low_a, low_b):
    return pl.pallas_call(
        place_kernel,
        grid_spec=pltpu.PrefetchScalarGridSpec(
            num_scalar_prefetch=1,
            grid=(TOK // SPAN,),
            in_specs=[pl.BlockSpec((SPAN, ROWS), lambda m, count: (m, 0))] + [whole((ROWS, 512))] * 2 + [whole((ROWS // 2, 512))] * 4,
            out_specs=pl.BlockSpec((SPAN, 512), lambda m, count: (m, 0)),
            scratch_shapes=[pltpu.VMEM((ROWS, 512), jnp.bfloat16)],
        ),
        out_shape=jax.ShapeDtypeStruct((TOK, 512), jnp.bfloat16),
        compiler_params=params(62),
        name="place",
    )(count, hot, own, other, full_a, full_b, low_a, low_b)


def branch(inputs, out_grad, router_score, route_index, block_count, w_in, w_out):
    picked = route_index[0]
    own_count = block_count[0]
    seq = lax.axis_index("seq")
    z = lax.axis_index("tensor")
    c = seq % 2
    y = (seq // 2) % SIDE
    x = seq // (2 * SIDE)

    w_out_t = w_out.T
    half = w_in.shape[1] // 2
    other_in, other_out = swap(w_in), swap(w_out_t)
    par_count = swap(block_count)

    xg, s_own = pick(
        block_count, route_index, router_score[None, :], inputs, out_grad
    )
    z_own = zdir(xg)
    xg_par = swap(xg)
    s_par = swap(s_own)
    z_par = zdir(xg_par)
    z_two = zdir(z_own)
    far_par = swap(z_own)
    far_own = swap(z_par)
    two_par = swap(z_two)
    own_rows = (xg, z_own, far_own, z_two)
    par_rows = (xg_par, z_par, far_par, two_par)

    def cut(w):
        return lax.dynamic_slice_in_dim(w, c * half, half, axis=1)

    def joined(w, other):
        a, b = cut(w), cut(other)
        return jnp.where(c == 0, jnp.concatenate([a, b], 0), jnp.concatenate([b, a], 0))

    s = jnp.stack([joined(w_in, other_in), joined(w_out_t, other_out)])
    p_f, p_b = hop(s, 1, 0), hop(s, -1, 0)
    y0f, y0b = hop(s, 1, 1), hop(s, -1, 1)
    h_in, h_out = hop(p_f[0], 1, 0), hop(p_b[1], -1, 0)
    r = jnp.concatenate([p_f[:1], p_b[:1], p_f[1:], p_b[1:]], 0)
    yrf, yrb = hop(r, 1, 1), hop(r, -1, 1)
    h = jnp.stack([h_in, h_out])
    yhf, yhb = hop(h, 1, 1), hop(h, -1, 1)
    a_in, a_out = hop(y0f[0], 1, 1), hop(y0b[1], -1, 1)
    r_in, r_out = hop(yrf[:2], 1, 1), hop(yrb[2:], -1, 1)
    low, high = yhf[0], yhb[1]
    b_in, b_out = hop(low, 1, 1), hop(high, -1, 1)

    rels = jnp.array(RELS, jnp.int32)
    grid_1 = jnp.tile(rels, SIDE)
    grid_2 = jnp.repeat(rels, SIDE)
    px = (x + jnp.where(c == 0, grid_1, grid_2)) % SIDE
    py = (y + jnp.where(c == 0, grid_2, grid_1)) % SIDE
    at = jnp.arange(CHIPS, dtype=jnp.int32)
    where = px * SIDE + py
    inverse = jnp.sum(jnp.where(where[None, :] == at[:, None], at[None, :], 0), axis=1)
    near = jnp.where(c == 0, 3, 1)
    order = jnp.stack([2 * jnp.ones_like(z), jnp.ones_like(z), 3 * jnp.ones_like(z), 0 * z])
    came = jnp.stack([0 * z, near, 4 - near, 2 * jnp.ones_like(z)])
    meta = jnp.concatenate(
        [px, py, inverse, block_count, par_count, (z + order) % SIDE, (z + came) % SIDE]
    ).astype(jnp.int32)

    pieces = (s, p_f, p_b, h_in, h_out, y0f, y0b, yrf, yrb, yhf, yhb)
    pieces = pieces + (a_in, r_in, b_in, a_out, r_out, b_out)
    o_par, o_par_0, score_par = half_stage(1, meta, par_rows, s_par, pieces)
    other = swap(o_par)
    other_0 = swap(o_par_0)
    score_other = swap(score_par[:, 0])
    o_own, o_own_0, score_own = half_stage(0, meta, own_rows, s_own, pieces)

    mid = ROWS // 2

    def both(k, a, b, extra=None):
        total = o_own[k, a:b].astype(jnp.float32) + other[k, a:b].astype(jnp.float32)
        if extra is not None:
            total = total + extra.astype(jnp.float32)
        return total.astype(jnp.bfloat16)

    through_f = zhop(both(0, 0, mid), 1)
    through_b = zhop(both(0, mid, ROWS), -1)
    low_b = zhop(both(1, mid, ROWS), 1)
    low_a = zhop(both(2, 0, mid), -1)

    row_scores = score_own[:, 0] + score_other
    up_one, down_one = zhop(row_scores, 1), zhop(row_scores, -1)
    row_scores = (row_scores + zhop(row_scores, 2)) + (up_one + down_one)

    full_a = zhop(both(1, 0, mid, through_f), 1)
    full_b = zhop(both(2, mid, ROWS, through_b), -1)
    hot = marks(route_index)
    input_grad = place(block_count, hot, o_own_0, other_0, full_a, full_b, low_a, low_b)
    is_mine = jnp.arange(ROWS, dtype=jnp.int32) < own_count * BLK
    mine_scores = jnp.where(is_mine, row_scores, 0.0)
    score_grad = jnp.zeros(router_score.shape, jnp.float32)
    score_grad = score_grad.at[picked].set(
        mine_scores, mode="promise_in_bounds", unique_indices=True
    )
    return (input_grad, score_grad)


def solution(mesh):
    placed = (
        P("seq", "tensor"),
        P("seq", "tensor"),
        P("seq"),
        P("seq", None),
        P("seq"),
        P("seq", "tensor"),
        P("tensor", "seq"),
    )
    return jax.shard_map(
        branch,
        mesh=mesh,
        in_specs=placed,
        out_specs=(P("seq", "tensor"), P("seq")),
        check_vma=False,
    )
```

```python
import functools

import jax
import jax.numpy as jnp
from jax import lax
from jax.experimental import pallas as pl
from jax.experimental.pallas import tpu as pltpu
from jax.sharding import PartitionSpec as P


BLK = 128
SIDE = 4
CHIPS = SIDE * SIDE

gelu_coeff = 0.7978845608028654
cubic_coeff = 0.044715

RELS = (0, -1, 1, 2)


def gelu_pair(values):
    square = values * values
    inner = values * (gelu_coeff + gelu_coeff * cubic_coeff * square)
    h = 0.5 * jnp.tanh(inner) + 0.5
    forward = values * h
    bend = values * (2.0 * gelu_coeff + 6.0 * gelu_coeff * cubic_coeff * square)
    slope = h + h * ((1.0 - h) * bend)
    return (forward, slope)


def seq_pairs(target):
    pairs = []
    for x in range(SIDE):
        for y in range(SIDE):
            for c in range(2):
                tx, ty, tc = target(x, y, c)
                pairs.append((((x * SIDE) + y) * 2 + c, ((tx % SIDE) * SIDE + ty % SIDE) * 2 + tc))
    return pairs


def ring(step, phase):
    return seq_pairs(lambda x, y, c: (x + step, y, c) if (c == phase) else (x, y + step, c))


SWAP = seq_pairs(lambda x, y, c: (x, y, 1 - c))


def swap(value):
    return lax.ppermute(value, "seq", SWAP)


def hop(value, step, phase):
    return lax.ppermute(value, "seq", ring(step, phase))


ZPAIRS = []
for z_at in range(SIDE):
    for s_at in range(2 * CHIPS):
        to = (z_at + (1 if s_at % 2 == 0 else -1)) % SIDE
        ZPAIRS.append((s_at * SIDE + z_at, s_at * SIDE + to))


def zdir(value):
    return lax.ppermute(value, ("seq", "tensor"), ZPAIRS)


def zhop(value, step):
    return lax.ppermute(value, "tensor", [(i, (i + step) % SIDE) for i in range(SIDE)])


TILE = 256
ROWS = 512
TOK = 4096
DOT = functools.partial(lax.dot_general, preferred_element_type=jnp.float32)
NN = (((1,), (0,)), ((), ()))
NT = (((1,), (1,)), ((), ()))
ANY = pl.BlockSpec(memory_space=pl.ANY)
HBM = pl.BlockSpec(memory_space=pltpu.MemorySpace.HBM)


def params(mib):
    return pltpu.CompilerParams(vmem_limit_bytes=mib << 20)


VMEM = pl.BlockSpec(memory_space=pltpu.MemorySpace.VMEM)
SMEM = pl.BlockSpec(memory_space=pltpu.MemorySpace.SMEM)


def on_chip(value):
    return pltpu.with_memory_space_constraint(value, pltpu.MemorySpace.VMEM)


def off_chip(value):
    return pltpu.with_memory_space_constraint(value, pltpu.MemorySpace.HBM)


def whole(shape):
    return pl.BlockSpec(shape, lambda m, meta: (0,) * len(shape))


def pick_kernel(count, idx_hbm, score_hbm, x_hbm, g_hbm, out, s_out, idx, score, xv, gv, hot, sems):
    small = [
        pltpu.make_async_copy(idx_hbm, idx, sems.at[2]),
        pltpu.make_async_copy(score_hbm, score, sems.at[3]),
    ]
    copies = [
        pltpu.make_async_copy(x_hbm, xv, sems.at[0]),
        pltpu.make_async_copy(g_hbm, gv, sems.at[1]),
    ]
    for copy in small + copies:
        copy.start()
    for copy in small:
        copy.wait()
    column = jnp.broadcast_to(idx[...], (BLK, ROWS)).T
    for r in range(ROWS // BLK):

        @pl.when(r < count[0])
        def _(r=r):
            at = jnp.broadcast_to(column[r * BLK : (r + 1) * BLK, :1], (BLK, TOK))
            same = lax.broadcasted_iota(jnp.int32, (BLK, TOK), 1) == at
            hot[r * BLK : (r + 1) * BLK, :] = jnp.where(same, 1.0, 0.0).astype(jnp.bfloat16)
            s_out[r * BLK : (r + 1) * BLK, :] = jnp.sum(
                jnp.where(same, score[...], 0.0), axis=1, keepdims=True
            )

    for k, (copy, rows) in enumerate(zip(copies, (xv, gv))):
        copy.wait()

        @pl.when(count[0] <= 2)
        def _(k=k, rows=rows):
            at = pl.ds(0, TILE)
            out[k, at, :] = DOT(hot[at, :], rows[...], NN).astype(jnp.bfloat16)

        @pl.when(count[0] > 2)
        def _(k=k, rows=rows):
            out[k] = DOT(hot[...], rows[...], NN).astype(jnp.bfloat16)


def pick(count, idx, score, inputs, out_grad):
    return pl.pallas_call(
        pick_kernel,
        grid_spec=pltpu.PrefetchScalarGridSpec(
            num_scalar_prefetch=1,
            grid=(1,),
            in_specs=[HBM] * 4,
            out_specs=[whole((2, ROWS, 512)), whole((ROWS, 1))],
            scratch_shapes=[
                pltpu.VMEM((1, ROWS), jnp.int32),
                pltpu.VMEM((1, TOK), jnp.float32),
                pltpu.VMEM((TOK, 512), jnp.bfloat16),
                pltpu.VMEM((TOK, 512), jnp.bfloat16),
                pltpu.VMEM((ROWS, TOK), jnp.bfloat16),
                pltpu.SemaphoreType.DMA((4,)),
            ],
        ),
        out_shape=[
            jax.ShapeDtypeStruct((2, ROWS, 512), jnp.bfloat16),
            jax.ShapeDtypeStruct((ROWS, 1), jnp.float32),
        ],
        compiler_params=params(18),
        name="pick",
    )(count, idx, score, inputs, out_grad)


def positions():
    seq, z = lax.axis_index("seq"), lax.axis_index("tensor")
    c, y, x = seq & 1, (seq >> 1) & 3, seq >> 3
    quarters, blocks, turns = [], [], []
    for k in range(CHIPS):
        first, second = RELS[k % SIDE], RELS[k // SIDE]
        px = (x + jnp.where(c == 0, first, second) + SIDE) & 3
        rel = (px - z + SIDE) & 3
        turn = jnp.where(rel == 0, 3, jnp.where(rel == 1, 1, jnp.where(rel == 2, 0, 2)))
        quarters.append(px)
        blocks.append((y + jnp.where(c == 0, second, first) + SIDE) & 3)
        turns.append(turn)
    near = jnp.where(c == 0, 3, 1)
    return quarters, blocks, turns, (z, (z + near) & 3, (z - near + SIDE) & 3, (z + 2) & 3)


def half_kernel(count, *refs):
    rows, scale_ref = refs[:4], refs[4]
    quarters, blocks, turns, came = positions()
    (sw, p_f, p_b, h_in, h_out, y0f, y0b, yrf, yrb, yhf, yhb) = refs[5:16]
    last = (refs[16:19], refs[19:22])
    out, score, rv, hg = refs[22:]

    lines = []
    for w in range(2):
        line = [sw.at[w], p_f.at[w], p_b.at[w], (h_in, h_out)[w]]
        for y0, yr, yh in ((y0f, yrf, yhf), (y0b, yrb, yhb)):
            line += [y0.at[w], yr.at[2 * w], yr.at[2 * w + 1], yh.at[w]]
        lines.append(line + [last[w][0], last[w][1].at[0], last[w][1].at[1], last[w][2]])

    def weights(w, cols):
        return jnp.concatenate([piece[:, cols] for piece in lines[w]], axis=0)

    def columns(which):
        parts = []
        for k in range(CHIPS):
            lanes = pl.ds(pl.multiple_of(blocks[k] * BLK, BLK), BLK)
            parts.append(rv[which, quarters[k], :, lanes])
        return jnp.concatenate(parts, axis=1)

    @pl.loop(0, (count[0] + 1) // 2)
    def _(tile):
        at = pl.ds(pl.multiple_of(tile * TILE, TILE), TILE)
        for r in range(SIDE):
            rv[:, came[r]] = rows[r][:, at, :]
        xs, gs, scale = columns(0), columns(1), scale_ref[at, :]
        total = None
        for n in range(4):
            cols = pl.ds(n * 256, 256)
            hidden = DOT(xs, weights(0, cols), NN)
            upstream = DOT(gs, weights(1, cols), NN)
            forward, slope = gelu_pair(hidden)
            active = forward.astype(jnp.bfloat16).astype(jnp.float32)
            term = jnp.sum(upstream * active, axis=1, keepdims=True)
            total = term if total is None else total + term
            hg[:, cols] = (scale * upstream * slope).astype(jnp.bfloat16)
        score[:, at] = jnp.broadcast_to(total, (TILE, BLK)).T[:1]
        for k in range(0, CHIPS, 2):
            pair = jnp.concatenate([lines[0][k][...], lines[0][k + 1][...]], axis=0)
            result = DOT(hg[...], pair, NT).astype(jnp.bfloat16)
            for i in range(2):
                lanes = pl.ds(pl.multiple_of(blocks[k + i] * BLK, BLK), BLK)
                out[turns[k + i], at, lanes] = result[:, i * BLK : (i + 1) * BLK]


def half_stage(count, rows, s, pieces):
    return pl.pallas_call(
        half_kernel,
        in_specs=[SMEM] + [VMEM] * 22,
        out_specs=[VMEM, VMEM],
        scratch_shapes=[
            pltpu.VMEM((2, SIDE, TILE, 512), jnp.bfloat16),
            pltpu.VMEM((TILE, 1024), jnp.bfloat16),
        ],
        out_shape=[
            pltpu.VMEM((SIDE, ROWS, 512), jnp.bfloat16),
            pltpu.VMEM((1, ROWS), jnp.float32),
        ],
        compiler_params=params(12),
        name="half_stage",
    )(count, *[on_chip(v) for v in (*rows, s, *pieces)])


def marks_kernel(count, idx, scores, out, score_out):
    lane = lax.broadcasted_iota(jnp.int32, (1, ROWS), 1)
    value = jnp.where(lane < count[0] * BLK, scores[...], 0.0)
    terms = []
    for _ in range(3):
        terms.append(value.astype(jnp.bfloat16))
        value = value - terms[-1].astype(jnp.float32)
    terms = jnp.concatenate(
        [jnp.broadcast_to(term.astype(jnp.float32), (8, ROWS)) for term in terms], axis=0
    ).astype(jnp.bfloat16)
    for t in range(TOK // ROWS):
        here = pl.ds(t * ROWS, ROWS)
        token = lax.broadcasted_iota(jnp.int32, (ROWS, ROWS), 0) + t * ROWS
        hot = jnp.where(token == jnp.broadcast_to(idx[...], (ROWS, ROWS)), 1.0, 0.0)
        hot = hot.astype(jnp.bfloat16)
        out[here, :] = hot
        found = DOT(terms, hot, NT)
        score_out[:, here] = found[:1] + found[8:9] + found[16:17]


def marks(count, idx, scores):
    return pl.pallas_call(
        marks_kernel,
        in_specs=[SMEM, VMEM, VMEM],
        out_specs=[VMEM, VMEM],
        out_shape=[
            pltpu.VMEM((TOK, ROWS), jnp.bfloat16),
            jax.ShapeDtypeStruct((1, TOK), jnp.float32),
        ],
        compiler_params=params(8),
        name="marks",
    )(count, idx, scores)


def place_kernel(count, hot, own, other, full_a, full_b, low_a, low_b, out, rows, done, sems):
    mid = ROWS // 2
    for at, parts in ((0, (full_a, low_a)), (mid, (full_b, low_b))):
        here = pl.ds(at, mid)
        total = own[3, here, :].astype(jnp.float32) + other[3, here, :].astype(jnp.float32)
        for part in parts:
            total = total + part[...].astype(jnp.float32)
        at_row = lax.broadcasted_iota(jnp.int32, (mid, 512), 0) + at
        total = jnp.where(at_row < count[0] * BLK, total, 0.0)
        rows[here, :] = total.astype(jnp.bfloat16)
    copies = []
    for t in range(TOK // ROWS):
        here = pl.ds(t * ROWS, ROWS)
        done[here, :] = DOT(hot[here, :], rows[...], NN).astype(jnp.bfloat16)
        copies.append(pltpu.make_async_copy(done.at[here], out.at[here], sems.at[t]))
        copies[-1].start()
    for copy in copies:
        copy.wait()


def place(count, hot, own, other, full_a, full_b, low_a, low_b):
    held = [on_chip(v) for v in (hot, own, other, full_a, full_b, low_a, low_b)]
    return pl.pallas_call(
        place_kernel,
        in_specs=[SMEM] + [VMEM] * 7,
        out_specs=HBM,
        scratch_shapes=[
            pltpu.VMEM((ROWS, 512), jnp.bfloat16),
            pltpu.VMEM((TOK, 512), jnp.bfloat16),
            pltpu.SemaphoreType.DMA((TOK // ROWS,)),
        ],
        out_shape=jax.ShapeDtypeStruct((TOK, 512), jnp.bfloat16),
        compiler_params=params(12),
        name="place",
    )(count, *held)


def branch(inputs, out_grad, router_score, route_index, block_count, w_in, w_out):
    seq = lax.axis_index("seq")
    c = seq % 2

    w_out_t = w_out.T
    half = w_in.shape[1] // 2
    other_in, other_out = swap(w_in), swap(w_out_t)
    par_count = swap(block_count)

    xg, s_own = pick(
        block_count,
        *[off_chip(v) for v in (route_index, router_score[None, :], inputs, out_grad)],
    )
    z_own = zdir(xg)
    xg_par = swap(xg)
    s_par = swap(s_own)
    z_par = zdir(xg_par)
    z_two = zdir(z_own)
    far_par = swap(z_own)
    far_own = swap(z_par)
    two_par = swap(z_two)
    own_rows = (xg, z_own, far_own, z_two)
    par_rows = (xg_par, z_par, far_par, two_par)

    def cut(w):
        return lax.dynamic_slice_in_dim(w, c * half, half, axis=1)

    def joined(w, other):
        a, b = cut(w), cut(other)
        return jnp.where(c == 0, jnp.concatenate([a, b], 0), jnp.concatenate([b, a], 0))

    s = jnp.stack([joined(w_in, other_in), joined(w_out_t, other_out)])
    p_f, p_b = hop(s, 1, 0), hop(s, -1, 0)
    y0f, y0b = hop(s, 1, 1), hop(s, -1, 1)
    h_in, h_out = hop(p_f[0], 1, 0), hop(p_b[1], -1, 0)
    r = jnp.concatenate([p_f[:1], p_b[:1], p_f[1:], p_b[1:]], 0)
    yrf, yrb = hop(r, 1, 1), hop(r, -1, 1)
    h = jnp.stack([h_in, h_out])
    yhf, yhb = hop(h, 1, 1), hop(h, -1, 1)
    a_in, a_out = hop(y0f[0], 1, 1), hop(y0b[1], -1, 1)
    r_in, r_out = hop(yrf[:2], 1, 1), hop(yrb[2:], -1, 1)
    low, high = yhf[0], yhb[1]
    b_in, b_out = hop(low, 1, 1), hop(high, -1, 1)

    pieces = (s, p_f, p_b, h_in, h_out, y0f, y0b, yrf, yrb, yhf, yhb)
    pieces = pieces + (a_in, r_in, b_in, a_out, r_out, b_out)
    o_par, score_par = half_stage(par_count, par_rows, s_par, pieces)
    other = swap(o_par)
    score_other = swap(score_par)
    o_own, score_own = half_stage(block_count, own_rows, s_own, pieces)

    mid = ROWS // 2

    def both(k, a, b, extra=None):
        total = o_own[k, a:b].astype(jnp.float32) + other[k, a:b].astype(jnp.float32)
        if extra is not None:
            total = total + extra.astype(jnp.float32)
        return total.astype(jnp.bfloat16)

    through_f = zhop(both(0, 0, mid), 1)
    through_b = zhop(both(0, mid, ROWS), -1)
    low_b = zhop(both(1, mid, ROWS), 1)
    low_a = zhop(both(2, 0, mid), -1)

    row_scores = score_own + score_other
    up_one, down_one = zhop(row_scores, 1), zhop(row_scores, -1)
    row_scores = (row_scores + zhop(row_scores, 2)) + (up_one + down_one)

    full_a = zhop(both(1, 0, mid, through_f), 1)
    full_b = zhop(both(2, mid, ROWS, through_b), -1)
    hot, score_grad = marks(block_count, route_index, row_scores)
    input_grad = place(block_count, hot, o_own, other, full_a, full_b, low_a, low_b)
    return (input_grad, score_grad.reshape(router_score.shape))


def solution(mesh):
    placed = (
        P("seq", "tensor"),
        P("seq", "tensor"),
        P("seq"),
        P("seq", None),
        P("seq"),
        P("seq", "tensor"),
        P("tensor", "seq"),
    )
    return jax.shard_map(
        branch,
        mesh=mesh,
        in_specs=placed,
        out_specs=(P("seq", "tensor"), P("seq")),
        check_vma=False,
    )
```

```python
import functools

import jax
import jax.numpy as jnp
from jax import lax
from jax.experimental import pallas as pl
from jax.experimental.pallas import tpu as pltpu
from jax.sharding import PartitionSpec as P


BLK = 128
SIDE = 4
CHIPS = SIDE * SIDE

gelu_coeff = 0.7978845608028654
cubic_coeff = 0.044715

RELS = (0, -1, 1, 2)


def gelu_pair(values):
    square = values * values
    inner = values * (gelu_coeff + gelu_coeff * cubic_coeff * square)
    h = 0.5 * jnp.tanh(inner) + 0.5
    forward = values * h
    bend = values * (2.0 * gelu_coeff + 6.0 * gelu_coeff * cubic_coeff * square)
    slope = h + h * ((1.0 - h) * bend)
    return (forward, slope)


def seq_pairs(target):
    pairs = []
    for x in range(SIDE):
        for y in range(SIDE):
            for c in range(2):
                tx, ty, tc = target(x, y, c)
                pairs.append((((x * SIDE) + y) * 2 + c, ((tx % SIDE) * SIDE + ty % SIDE) * 2 + tc))
    return pairs


def ring(step, phase):
    return seq_pairs(lambda x, y, c: (x + step, y, c) if (c == phase) else (x, y + step, c))


SWAP = seq_pairs(lambda x, y, c: (x, y, 1 - c))


def swap(value):
    return lax.ppermute(value, "seq", SWAP)


def hop(value, step, phase):
    return lax.ppermute(value, "seq", ring(step, phase))


ZPAIRS = []
for z_at in range(SIDE):
    for s_at in range(2 * CHIPS):
        to = (z_at + (1 if s_at % 2 == 0 else -1)) % SIDE
        ZPAIRS.append((s_at * SIDE + z_at, s_at * SIDE + to))


def zdir(value):
    return lax.ppermute(value, ("seq", "tensor"), ZPAIRS)


def zhop(value, step):
    return lax.ppermute(value, "tensor", [(i, (i + step) % SIDE) for i in range(SIDE)])


TILE = 256
ROWS = 512
TOK = 4096
DOT = functools.partial(lax.dot_general, preferred_element_type=jnp.float32)
NN = (((1,), (0,)), ((), ()))
NT = (((1,), (1,)), ((), ()))
ANY = pl.BlockSpec(memory_space=pl.ANY)
HBM = pl.BlockSpec(memory_space=pltpu.MemorySpace.HBM)


def params(mib):
    return pltpu.CompilerParams(vmem_limit_bytes=mib << 20)


VMEM = pl.BlockSpec(memory_space=pltpu.MemorySpace.VMEM)
SMEM = pl.BlockSpec(memory_space=pltpu.MemorySpace.SMEM)


def on_chip(value):
    return pltpu.with_memory_space_constraint(value, pltpu.MemorySpace.VMEM)


def off_chip(value):
    return pltpu.with_memory_space_constraint(value, pltpu.MemorySpace.HBM)


def pick_kernel(count, idx_hbm, x_hbm, g_hbm, out, idx, xv, gv, hot, sems):
    first = pltpu.make_async_copy(idx_hbm, idx, sems.at[8])
    copies = []
    for k, (far, near) in enumerate(((x_hbm, xv), (g_hbm, gv))):
        parts = [pl.ds(t * (TOK // 4), TOK // 4) for t in range(4)]
        copies.append(
            [
                pltpu.make_async_copy(far.at[at], near.at[at], sems.at[4 * k + t])
                for t, at in enumerate(parts)
            ]
        )
    for copy in [first] + copies[0] + copies[1]:
        copy.start()
    first.wait()
    column = jnp.broadcast_to(idx[...], (BLK, ROWS)).T.astype(jnp.int16)
    lane = lax.broadcasted_iota(jnp.int32, (BLK, BLK), 1).astype(jnp.int16)
    one, none = jnp.ones((BLK, BLK), jnp.bfloat16), jnp.zeros((BLK, BLK), jnp.bfloat16)
    for r in range(ROWS // BLK):

        @pl.when(r < count[0])
        def _(r=r):
            here = slice(r * BLK, (r + 1) * BLK)
            for t in range(TOK // BLK):
                same = column[here, :] == lane + jnp.int16(t * BLK)
                hot[here, t * BLK : (t + 1) * BLK] = jnp.where(same, one, none)

    for k, (parts, rows) in enumerate(zip(copies, (xv, gv))):
        for copy in parts:
            copy.wait()

        @pl.when(count[0] <= 2)
        def _(k=k, rows=rows):
            at = pl.ds(0, TILE)
            out[k, at, :] = DOT(hot[at, :], rows[...], NN).astype(jnp.bfloat16)

        @pl.when(count[0] > 2)
        def _(k=k, rows=rows):
            out[k] = DOT(hot[...], rows[...], NN).astype(jnp.bfloat16)


def pick(count, idx, inputs, out_grad):
    return pl.pallas_call(
        pick_kernel,
        in_specs=[SMEM, HBM, HBM, HBM],
        out_specs=VMEM,
        scratch_shapes=[
            pltpu.VMEM((1, ROWS), jnp.int32),
            pltpu.VMEM((TOK, 512), jnp.bfloat16),
            pltpu.VMEM((TOK, 512), jnp.bfloat16),
            pltpu.VMEM((ROWS, TOK), jnp.bfloat16),
            pltpu.SemaphoreType.DMA((9,)),
        ],
        out_shape=pltpu.VMEM((2, ROWS, 512), jnp.bfloat16),
        compiler_params=params(18),
        name="pick",
    )(count, *[off_chip(v) for v in (idx, inputs, out_grad)])


def scale_kernel(count, idx, score, out):
    column = jnp.broadcast_to(idx[...], (BLK, ROWS)).T
    for r in range(ROWS // BLK):

        @pl.when(r < count[0])
        def _(r=r):
            here = slice(r * BLK, (r + 1) * BLK)
            at = jnp.broadcast_to(column[here, :1], (BLK, TOK))
            same = lax.broadcasted_iota(jnp.int32, (BLK, TOK), 1) == at
            out[here, :] = jnp.sum(jnp.where(same, score[...], 0.0), axis=1, keepdims=True)


def scale(count, idx, score):
    return pl.pallas_call(
        scale_kernel,
        in_specs=[SMEM, VMEM, VMEM],
        out_specs=VMEM,
        out_shape=pltpu.VMEM((ROWS, 1), jnp.float32),
        compiler_params=params(8),
        name="scale",
    )(count, idx, score)


def positions():
    seq, z = lax.axis_index("seq"), lax.axis_index("tensor")
    c, y, x = seq & 1, (seq >> 1) & 3, seq >> 3
    quarters, blocks, turns = [], [], []
    for k in range(CHIPS):
        first, second = RELS[k % SIDE], RELS[k // SIDE]
        px = (x + jnp.where(c == 0, first, second) + SIDE) & 3
        rel = (px - z + SIDE) & 3
        turn = jnp.where(rel == 0, 3, jnp.where(rel == 1, 1, jnp.where(rel == 2, 0, 2)))
        quarters.append(px)
        blocks.append((y + jnp.where(c == 0, second, first) + SIDE) & 3)
        turns.append(turn)
    near = jnp.where(c == 0, 3, 1)
    return quarters, blocks, turns, (z, (z + near) & 3, (z - near + SIDE) & 3, (z + 2) & 3)


def half_kernel(tiles, count, *refs):
    rows, scale_ref = refs[:4], refs[4]
    quarters, blocks, turns, came = positions()
    (sw, p_f, p_b, h_in, h_out, y0f, y0b, yrf, yrb, yhf, yhb) = refs[5:16]
    last = (refs[16:19], refs[19:22])
    before, (out, score, rv, hg) = refs[22:-4], refs[-4:]
    if before:
        score[...] = before[0][...]

    lines = []
    for w in range(2):
        line = [sw.at[w], p_f.at[w], p_b.at[w], (h_in, h_out)[w]]
        for y0, yr, yh in ((y0f, yrf, yhf), (y0b, yrb, yhb)):
            line += [y0.at[w], yr.at[2 * w], yr.at[2 * w + 1], yh.at[w]]
        lines.append(line + [last[w][0], last[w][1].at[0], last[w][1].at[1], last[w][2]])

    def weights(w, cols):
        return jnp.concatenate([piece[:, cols] for piece in lines[w]], axis=0)

    def columns(which):
        parts = []
        for k in range(CHIPS):
            lanes = pl.ds(pl.multiple_of(blocks[k] * BLK, BLK), BLK)
            parts.append(rv[which, quarters[k], :, lanes])
        return jnp.concatenate(parts, axis=1)

    @pl.loop(tiles[0], jnp.minimum((count[0] + 1) // 2, tiles[1]))
    def _(tile):
        at = pl.ds(pl.multiple_of(tile * TILE, TILE), TILE)
        to = pl.ds(pl.multiple_of((tile - tiles[0]) * TILE, TILE), TILE)
        for r in range(SIDE):
            rv[:, came[r]] = rows[r][:, at, :]
        xs, gs, scale = columns(0), columns(1), scale_ref[at, :]
        total = None

        def products(n):
            cols = pl.ds(n * 256, 256)
            return DOT(xs, weights(0, cols), NN), DOT(gs, weights(1, cols), NN)

        ahead = products(0)
        for n in range(4):
            cols = pl.ds(n * 256, 256)
            hidden, upstream = ahead
            if n < 3:
                ahead = products(n + 1)
            forward, slope = gelu_pair(hidden)
            active = forward.astype(jnp.bfloat16).astype(jnp.float32)
            term = jnp.sum(upstream * active, axis=1, keepdims=True)
            total = term if total is None else total + term
            hg[:, cols] = (scale * upstream * slope).astype(jnp.bfloat16)
        score[:, at] = jnp.broadcast_to(total, (TILE, BLK)).T[:1]
        for k in range(0, CHIPS, 2):
            pair = jnp.concatenate([lines[0][k][...], lines[0][k + 1][...]], axis=0)
            result = DOT(hg[...], pair, NT).astype(jnp.bfloat16)
            for i in range(2):
                lanes = pl.ds(pl.multiple_of(blocks[k + i] * BLK, BLK), BLK)
                out[turns[k + i], to, lanes] = result[:, i * BLK : (i + 1) * BLK]


def half_stage(tiles, count, rows, s, pieces, before=()):
    return pl.pallas_call(
        functools.partial(half_kernel, tiles),
        in_specs=[SMEM] + [VMEM] * (22 + len(before)),
        out_specs=[VMEM, VMEM],
        scratch_shapes=[
            pltpu.VMEM((2, SIDE, TILE, 512), jnp.bfloat16),
            pltpu.VMEM((TILE, 1024), jnp.bfloat16),
        ],
        out_shape=[
            pltpu.VMEM((SIDE, (tiles[1] - tiles[0]) * TILE, 512), jnp.bfloat16),
            pltpu.VMEM((1, ROWS), jnp.float32),
        ],
        compiler_params=params(12),
        name="half_stage",
    )(count, *[on_chip(v) for v in (*rows, s, *pieces, *before)])


def merge_kernel(turns, at, own, other, *refs):
    extra, outs = refs[: -len(turns)], refs[-len(turns) :]
    for k, out in zip(turns, outs):
        total = own[k].astype(jnp.float32) + other[k, at : at + TILE].astype(jnp.float32)
        for part in extra:
            total = total + part[...].astype(jnp.float32)
        out[...] = total.astype(jnp.bfloat16)


def merge(turns, at, *parts):
    return pl.pallas_call(
        functools.partial(merge_kernel, turns, at),
        in_specs=[VMEM] * len(parts),
        out_specs=[VMEM] * len(turns),
        out_shape=[pltpu.VMEM((TILE, 512), jnp.bfloat16)] * len(turns),
        compiler_params=params(4),
        name="merge",
    )(*[on_chip(v) for v in parts])


def marks_kernel(count, idx, scores, out, score_out):
    lane = lax.broadcasted_iota(jnp.int32, (1, ROWS), 1)
    value = jnp.where(lane < count[0] * BLK, scores[...], 0.0)
    terms = []
    for _ in range(3):
        terms.append(value.astype(jnp.bfloat16))
        value = value - terms[-1].astype(jnp.float32)
    terms = jnp.concatenate(
        [jnp.broadcast_to(term.astype(jnp.float32), (8, ROWS)) for term in terms], axis=0
    ).astype(jnp.bfloat16)
    for t in range(TOK // ROWS):
        here = pl.ds(t * ROWS, ROWS)
        token = lax.broadcasted_iota(jnp.int32, (ROWS, ROWS), 0) + t * ROWS
        hot = jnp.where(token == jnp.broadcast_to(idx[...], (ROWS, ROWS)), 1.0, 0.0)
        hot = hot.astype(jnp.bfloat16)
        out[here, :] = hot
        found = DOT(terms, hot, NT)
        score_out[:, here] = found[:1] + found[8:9] + found[16:17]


def marks(count, idx, scores):
    return pl.pallas_call(
        marks_kernel,
        in_specs=[SMEM, VMEM, VMEM],
        out_specs=[VMEM, VMEM],
        out_shape=[
            pltpu.VMEM((TOK, ROWS), jnp.bfloat16),
            jax.ShapeDtypeStruct((1, TOK), jnp.float32),
        ],
        compiler_params=params(8),
        name="marks",
    )(count, idx, scores)


def place_kernel(count, hot, own_a, own_b, other, full_a, full_b, low_a, low_b, out, rows, done, sems):
    mid = ROWS // 2
    for at, own, parts in ((0, own_a, (full_a, low_a)), (mid, own_b, (full_b, low_b))):
        here = pl.ds(at, mid)
        total = own[3].astype(jnp.float32) + other[3, here, :].astype(jnp.float32)
        for part in parts:
            total = total + part[...].astype(jnp.float32)
        at_row = lax.broadcasted_iota(jnp.int32, (mid, 512), 0) + at
        total = jnp.where(at_row < count[0] * BLK, total, 0.0)
        rows[here, :] = total.astype(jnp.bfloat16)
    copies = []
    for t in range(TOK // ROWS):
        here = pl.ds(t * ROWS, ROWS)
        done[here, :] = DOT(hot[here, :], rows[...], NN).astype(jnp.bfloat16)
        copies.append(pltpu.make_async_copy(done.at[here], out.at[here], sems.at[t]))
        copies[-1].start()
    for copy in copies:
        copy.wait()


def place(count, hot, own_a, own_b, other, full_a, full_b, low_a, low_b):
    held = [on_chip(v) for v in (hot, own_a, own_b, other, full_a, full_b, low_a, low_b)]
    return pl.pallas_call(
        place_kernel,
        in_specs=[SMEM] + [VMEM] * 8,
        out_specs=HBM,
        scratch_shapes=[
            pltpu.VMEM((ROWS, 512), jnp.bfloat16),
            pltpu.VMEM((TOK, 512), jnp.bfloat16),
            pltpu.SemaphoreType.DMA((TOK // ROWS,)),
        ],
        out_shape=jax.ShapeDtypeStruct((TOK, 512), jnp.bfloat16),
        compiler_params=params(12),
        name="place",
    )(count, *held)


def branch(inputs, out_grad, router_score, route_index, block_count, w_in, w_out):
    seq = lax.axis_index("seq")
    c = seq % 2

    w_out_t = w_out.T
    half = w_in.shape[1] // 2
    other_in, other_out = swap(w_in), swap(w_out_t)
    par_count = swap(block_count)

    xg = pick(block_count, route_index, inputs, out_grad)
    s_own = scale(block_count, route_index, router_score[None, :])
    z_own = zdir(xg)
    xg_par = swap(xg)
    s_par = swap(s_own)
    z_par = zdir(xg_par)
    z_two = zdir(z_own)
    far_par = swap(z_own)
    far_own = swap(z_par)
    two_par = swap(z_two)
    own_rows = (xg, z_own, far_own, z_two)
    par_rows = (xg_par, z_par, far_par, two_par)

    def cut(w):
        return lax.dynamic_slice_in_dim(w, c * half, half, axis=1)

    def joined(w, other):
        a, b = cut(w), cut(other)
        return jnp.where(c == 0, jnp.concatenate([a, b], 0), jnp.concatenate([b, a], 0))

    s = jnp.stack([joined(w_in, other_in), joined(w_out_t, other_out)])
    p_f, p_b = hop(s, 1, 0), hop(s, -1, 0)
    y0f, y0b = hop(s, 1, 1), hop(s, -1, 1)
    h_in, h_out = hop(p_f[0], 1, 0), hop(p_b[1], -1, 0)
    r = jnp.concatenate([p_f[:1], p_b[:1], p_f[1:], p_b[1:]], 0)
    yrf, yrb = hop(r, 1, 1), hop(r, -1, 1)
    h = jnp.stack([h_in, h_out])
    yhf, yhb = hop(h, 1, 1), hop(h, -1, 1)
    a_in, a_out = hop(y0f[0], 1, 1), hop(y0b[1], -1, 1)
    r_in, r_out = hop(yrf[:2], 1, 1), hop(yrb[2:], -1, 1)
    low, high = yhf[0], yhb[1]
    b_in, b_out = hop(low, 1, 1), hop(high, -1, 1)

    pieces = (s, p_f, p_b, h_in, h_out, y0f, y0b, yrf, yrb, yhf, yhb)
    pieces = pieces + (a_in, r_in, b_in, a_out, r_out, b_out)
    o_par, score_par = half_stage((0, 2), par_count, par_rows, s_par, pieces)
    other = swap(o_par)
    score_other = swap(score_par)
    o_a, score_a = half_stage((0, 1), block_count, own_rows, s_own, pieces)
    o_b, score_own = half_stage((1, 2), block_count, own_rows, s_own, pieces, (score_a,))

    mid = ROWS // 2
    add_a, sent_a = merge((0, 2), 0, o_a, other)
    through_f, low_a = zhop(add_a, 1), zhop(sent_a, -1)
    add_b, sent_b = merge((0, 1), mid, o_b, other)
    through_b, low_b = zhop(add_b, -1), zhop(sent_b, 1)

    row_scores = score_own + score_other
    up_one, down_one = zhop(row_scores, 1), zhop(row_scores, -1)
    row_scores = (row_scores + zhop(row_scores, 2)) + (up_one + down_one)

    (more_a,) = merge((1,), 0, o_a, other, through_f)
    (more_b,) = merge((2,), mid, o_b, other, through_b)
    full_a, full_b = zhop(more_a, 1), zhop(more_b, -1)
    hot, score_grad = marks(block_count, route_index, row_scores)
    input_grad = place(block_count, hot, o_a, o_b, other, full_a, full_b, low_a, low_b)
    return (input_grad, score_grad.reshape(router_score.shape))


def solution(mesh):
    placed = (
        P("seq", "tensor"),
        P("seq", "tensor"),
        P("seq"),
        P("seq", None),
        P("seq"),
        P("seq", "tensor"),
        P("tensor", "seq"),
    )
    return jax.shard_map(
        branch,
        mesh=mesh,
        in_specs=placed,
        out_specs=(P("seq", "tensor"), P("seq")),
        check_vma=False,
    )
```

```python
import functools

import jax
import jax.numpy as jnp
from jax import lax
from jax.experimental import pallas as pl
from jax.experimental.pallas import tpu as pltpu
from jax.sharding import PartitionSpec as P


BLK = 128
SIDE = 4
CHIPS = SIDE * SIDE

gelu_coeff = 0.7978845608028654
cubic_coeff = 0.044715

RELS = (0, -1, 1, 2)


def gelu_pair(values):
    square = values * values
    inner = values * (gelu_coeff + gelu_coeff * cubic_coeff * square)
    h = 0.5 * jnp.tanh(inner) + 0.5
    forward = values * h
    bend = values * (2.0 * gelu_coeff + 6.0 * gelu_coeff * cubic_coeff * square)
    slope = h + h * ((1.0 - h) * bend)
    return (forward, slope)


def seq_pairs(target):
    pairs = []
    for x in range(SIDE):
        for y in range(SIDE):
            for c in range(2):
                tx, ty, tc = target(x, y, c)
                pairs.append((((x * SIDE) + y) * 2 + c, ((tx % SIDE) * SIDE + ty % SIDE) * 2 + tc))
    return pairs


def ring(step, phase):
    return seq_pairs(lambda x, y, c: (x + step, y, c) if (c == phase) else (x, y + step, c))


SWAP = seq_pairs(lambda x, y, c: (x, y, 1 - c))


def swap(value):
    return lax.ppermute(value, "seq", SWAP)


def hop(value, step, phase):
    return lax.ppermute(value, "seq", ring(step, phase))


ZPAIRS = []
for z_at in range(SIDE):
    for s_at in range(2 * CHIPS):
        to = (z_at + (1 if s_at % 2 == 0 else -1)) % SIDE
        ZPAIRS.append((s_at * SIDE + z_at, s_at * SIDE + to))


def zdir(value):
    return lax.ppermute(value, ("seq", "tensor"), ZPAIRS)


def zhop(value, step):
    return lax.ppermute(value, "tensor", [(i, (i + step) % SIDE) for i in range(SIDE)])


TILE = 256
ROWS = 512
TOK = 4096
DOT = functools.partial(lax.dot_general, preferred_element_type=jnp.float32)
NN = (((1,), (0,)), ((), ()))
NT = (((1,), (1,)), ((), ()))
ANY = pl.BlockSpec(memory_space=pl.ANY)
HBM = pl.BlockSpec(memory_space=pltpu.MemorySpace.HBM)


def params(mib):
    return pltpu.CompilerParams(vmem_limit_bytes=mib << 20)


VMEM = pl.BlockSpec(memory_space=pltpu.MemorySpace.VMEM)
SMEM = pl.BlockSpec(memory_space=pltpu.MemorySpace.SMEM)


def on_chip(value):
    return pltpu.with_memory_space_constraint(value, pltpu.MemorySpace.VMEM)


def off_chip(value):
    return pltpu.with_memory_space_constraint(value, pltpu.MemorySpace.HBM)


def pick_kernel(count, idx_hbm, x_hbm, g_hbm, out, idx, xv, gv, hot, sems):
    first = pltpu.make_async_copy(idx_hbm, idx, sems.at[8])
    copies = []
    for k, (far, near) in enumerate(((x_hbm, xv), (g_hbm, gv))):
        parts = [pl.ds(t * (TOK // 4), TOK // 4) for t in range(4)]
        copies.append(
            [
                pltpu.make_async_copy(far.at[at], near.at[at], sems.at[4 * k + t])
                for t, at in enumerate(parts)
            ]
        )
    for copy in [first] + copies[0] + copies[1]:
        copy.start()
    first.wait()
    column = jnp.broadcast_to(idx[...], (BLK, ROWS)).T.astype(jnp.int16)
    lane = lax.broadcasted_iota(jnp.int32, (BLK, BLK), 1).astype(jnp.int16)
    one, none = jnp.ones((BLK, BLK), jnp.bfloat16), jnp.zeros((BLK, BLK), jnp.bfloat16)
    for r in range(ROWS // BLK):

        @pl.when(r < count[0])
        def _(r=r):
            here = slice(r * BLK, (r + 1) * BLK)
            for t in range(TOK // BLK):
                same = column[here, :] == lane + jnp.int16(t * BLK)
                hot[here, t * BLK : (t + 1) * BLK] = jnp.where(same, one, none)

    for k, (parts, rows) in enumerate(zip(copies, (xv, gv))):
        for copy in parts:
            copy.wait()

        @pl.when(count[0] <= 2)
        def _(k=k, rows=rows):
            at = pl.ds(0, TILE)
            out[k, at, :] = DOT(hot[at, :], rows[...], NN).astype(jnp.bfloat16)

        @pl.when(count[0] > 2)
        def _(k=k, rows=rows):
            out[k] = DOT(hot[...], rows[...], NN).astype(jnp.bfloat16)


def pick(count, idx, inputs, out_grad):
    return pl.pallas_call(
        pick_kernel,
        in_specs=[SMEM, HBM, HBM, HBM],
        out_specs=VMEM,
        scratch_shapes=[
            pltpu.VMEM((1, ROWS), jnp.int32),
            pltpu.VMEM((TOK, 512), jnp.bfloat16),
            pltpu.VMEM((TOK, 512), jnp.bfloat16),
            pltpu.VMEM((ROWS, TOK), jnp.bfloat16),
            pltpu.SemaphoreType.DMA((9,)),
        ],
        out_shape=pltpu.VMEM((2, ROWS, 512), jnp.bfloat16),
        compiler_params=params(18),
        name="pick",
    )(count, *[off_chip(v) for v in (idx, inputs, out_grad)])


def scale_kernel(count, idx, score, out, column):
    column[...] = jnp.broadcast_to(idx[...], (BLK, ROWS)).T

    @pl.loop(0, count[0])
    def _(r):
        here = pl.ds(pl.multiple_of(r * BLK, BLK), BLK)
        at = jnp.broadcast_to(column[here, :1], (BLK, TOK))
        same = lax.broadcasted_iota(jnp.int32, (BLK, TOK), 1) == at
        out[here, :] = jnp.sum(jnp.where(same, score[...], 0.0), axis=1, keepdims=True)


def scale(count, idx, score):
    return pl.pallas_call(
        scale_kernel,
        in_specs=[SMEM, VMEM, VMEM],
        out_specs=VMEM,
        scratch_shapes=[pltpu.VMEM((ROWS, BLK), jnp.int32)],
        out_shape=pltpu.VMEM((ROWS, 1), jnp.float32),
        compiler_params=params(8),
        name="scale",
    )(count, idx, score)


def positions():
    seq, z = lax.axis_index("seq"), lax.axis_index("tensor")
    c, y, x = seq & 1, (seq >> 1) & 3, seq >> 3
    quarters, blocks, turns = [], [], []
    for k in range(CHIPS):
        first, second = RELS[k % SIDE], RELS[k // SIDE]
        px = (x + jnp.where(c == 0, first, second) + SIDE) & 3
        rel = (px - z + SIDE) & 3
        turn = jnp.where(rel == 0, 3, jnp.where(rel == 1, 1, jnp.where(rel == 2, 0, 2)))
        quarters.append(px)
        blocks.append((y + jnp.where(c == 0, second, first) + SIDE) & 3)
        turns.append(turn)
    near = jnp.where(c == 0, 3, 1)
    return quarters, blocks, turns, (z, (z + near) & 3, (z - near + SIDE) & 3, (z + 2) & 3)


def half_kernel(tiles, count, *refs):
    rows, scale_ref = refs[:4], refs[4]
    quarters, blocks, turns, came = positions()
    (sw, p_f, p_b, h_in, h_out, y0f, y0b, yrf, yrb, yhf, yhb) = refs[5:16]
    last = (refs[16:19], refs[19:22])
    before, (out, score, rv, hg) = refs[22:-4], refs[-4:]
    if before:
        score[...] = before[0][...]

    lines = []
    for w in range(2):
        line = [sw.at[w], p_f.at[w], p_b.at[w], (h_in, h_out)[w]]
        for y0, yr, yh in ((y0f, yrf, yhf), (y0b, yrb, yhb)):
            line += [y0.at[w], yr.at[2 * w], yr.at[2 * w + 1], yh.at[w]]
        lines.append(line + [last[w][0], last[w][1].at[0], last[w][1].at[1], last[w][2]])

    def weights(w, cols):
        return jnp.concatenate([piece[:, cols] for piece in lines[w]], axis=0)

    def columns(which):
        parts = []
        for k in range(CHIPS):
            lanes = pl.ds(pl.multiple_of(blocks[k] * BLK, BLK), BLK)
            parts.append(rv[which, quarters[k], :, lanes])
        return jnp.concatenate(parts, axis=1)

    @pl.loop(tiles[0], jnp.minimum((count[0] + 1) // 2, tiles[1]))
    def _(tile):
        at = pl.ds(pl.multiple_of(tile * TILE, TILE), TILE)
        to = pl.ds(pl.multiple_of((tile - tiles[0]) * TILE, TILE), TILE)
        for r in range(SIDE):
            rv[:, came[r]] = rows[r][:, at, :]
        xs, gs, scale = columns(0), columns(1), scale_ref[at, :]
        total = None

        def products(n):
            cols = pl.ds(n * 256, 256)
            return DOT(xs, weights(0, cols), NN), DOT(gs, weights(1, cols), NN)

        ahead = products(0)
        for n in range(4):
            cols = pl.ds(n * 256, 256)
            hidden, upstream = ahead
            if n < 3:
                ahead = products(n + 1)
            forward, slope = gelu_pair(hidden)
            active = forward.astype(jnp.bfloat16).astype(jnp.float32)
            term = jnp.sum(upstream * active, axis=1, keepdims=True)
            total = term if total is None else total + term
            hg[:, cols] = (scale * upstream * slope).astype(jnp.bfloat16)
        score[:, at] = jnp.broadcast_to(total, (TILE, BLK)).T[:1]
        for k in range(0, CHIPS, 2):
            pair = jnp.concatenate([lines[0][k][...], lines[0][k + 1][...]], axis=0)
            result = DOT(hg[...], pair, NT).astype(jnp.bfloat16)
            for i in range(2):
                lanes = pl.ds(pl.multiple_of(blocks[k + i] * BLK, BLK), BLK)
                out[turns[k + i], to, lanes] = result[:, i * BLK : (i + 1) * BLK]


def half_stage(tiles, count, rows, s, pieces, before=()):
    return pl.pallas_call(
        functools.partial(half_kernel, tiles),
        in_specs=[SMEM] + [VMEM] * (22 + len(before)),
        out_specs=[VMEM, VMEM],
        scratch_shapes=[
            pltpu.VMEM((2, SIDE, TILE, 512), jnp.bfloat16),
            pltpu.VMEM((TILE, 1024), jnp.bfloat16),
        ],
        out_shape=[
            pltpu.VMEM((SIDE, (tiles[1] - tiles[0]) * TILE, 512), jnp.bfloat16),
            pltpu.VMEM((1, ROWS), jnp.float32),
        ],
        compiler_params=params(12),
        name="half_stage",
    )(count, *[on_chip(v) for v in (*rows, s, *pieces, *before)])


def merge_kernel(turns, at, own, other, *refs):
    extra, outs = refs[: -len(turns)], refs[-len(turns) :]
    for k, out in zip(turns, outs):
        total = own[k].astype(jnp.float32) + other[k, at : at + TILE].astype(jnp.float32)
        for part in extra:
            total = total + part[...].astype(jnp.float32)
        out[...] = total.astype(jnp.bfloat16)


def merge(turns, at, *parts):
    return pl.pallas_call(
        functools.partial(merge_kernel, turns, at),
        in_specs=[VMEM] * len(parts),
        out_specs=[VMEM] * len(turns),
        out_shape=[pltpu.VMEM((TILE, 512), jnp.bfloat16)] * len(turns),
        compiler_params=params(4),
        name="merge",
    )(*[on_chip(v) for v in parts])


def marks_kernel(count, idx, scores, out, score_out):
    lane = lax.broadcasted_iota(jnp.int32, (1, ROWS), 1)
    value = jnp.where(lane < count[0] * BLK, scores[...], 0.0)
    terms = []
    for _ in range(3):
        terms.append(value.astype(jnp.bfloat16))
        value = value - terms[-1].astype(jnp.float32)
    terms = jnp.concatenate(
        [jnp.broadcast_to(term.astype(jnp.float32), (8, ROWS)) for term in terms], axis=0
    ).astype(jnp.bfloat16)
    for t in range(TOK // ROWS):
        here = pl.ds(t * ROWS, ROWS)
        token = lax.broadcasted_iota(jnp.int32, (ROWS, ROWS), 0) + t * ROWS
        hot = jnp.where(token == jnp.broadcast_to(idx[...], (ROWS, ROWS)), 1.0, 0.0)
        hot = hot.astype(jnp.bfloat16)
        out[here, :] = hot
        found = DOT(terms, hot, NT)
        score_out[:, here] = found[:1] + found[8:9] + found[16:17]


def marks(count, idx, scores):
    return pl.pallas_call(
        marks_kernel,
        in_specs=[SMEM, VMEM, VMEM],
        out_specs=[VMEM, VMEM],
        out_shape=[
            pltpu.VMEM((TOK, ROWS), jnp.bfloat16),
            jax.ShapeDtypeStruct((1, TOK), jnp.float32),
        ],
        compiler_params=params(8),
        name="marks",
    )(count, idx, scores)


def finished(count, at, own, other, full, low):
    total = own[3].astype(jnp.float32) + other[3, at : at + TILE].astype(jnp.float32)
    total = total + full[...].astype(jnp.float32) + low[...].astype(jnp.float32)
    at_row = lax.broadcasted_iota(jnp.int32, (TILE, 512), 0) + at
    return jnp.where(at_row < count[0] * BLK, total, 0.0).astype(jnp.bfloat16)


def early_kernel(count, hot, own, other, full, low, held, rows):
    rows[...] = finished(count, 0, own, other, full, low)
    for t in range(TOK // ROWS):
        here = pl.ds(t * ROWS, ROWS)
        held[here, :] = DOT(hot[here, :TILE], rows[...], NN).astype(jnp.bfloat16)


def place_kernel(count, hot, held, own, other, full, low, out, rows, done, sems):
    rows[...] = finished(count, TILE, own, other, full, low)
    copies = []
    for t in range(TOK // ROWS):
        here = pl.ds(t * ROWS, ROWS)
        total = DOT(hot[here, TILE:], rows[...], NN) + held[here, :].astype(jnp.float32)
        done[here, :] = total.astype(jnp.bfloat16)
        copies.append(pltpu.make_async_copy(done.at[here], out.at[here], sems.at[t]))
        copies[-1].start()
    for copy in copies:
        copy.wait()


def early(count, *parts):
    return pl.pallas_call(
        early_kernel,
        in_specs=[SMEM] + [VMEM] * 5,
        out_specs=VMEM,
        scratch_shapes=[pltpu.VMEM((TILE, 512), jnp.bfloat16)],
        out_shape=pltpu.VMEM((TOK, 512), jnp.bfloat16),
        compiler_params=params(4),
        name="early",
    )(count, *[on_chip(v) for v in parts])


def place(count, *parts):
    return pl.pallas_call(
        place_kernel,
        in_specs=[SMEM] + [VMEM] * 6,
        out_specs=HBM,
        scratch_shapes=[
            pltpu.VMEM((TILE, 512), jnp.bfloat16),
            pltpu.VMEM((TOK, 512), jnp.bfloat16),
            pltpu.SemaphoreType.DMA((TOK // ROWS,)),
        ],
        out_shape=jax.ShapeDtypeStruct((TOK, 512), jnp.bfloat16),
        compiler_params=params(12),
        name="place",
    )(count, *[on_chip(v) for v in parts])


def branch(inputs, out_grad, router_score, route_index, block_count, w_in, w_out):
    seq = lax.axis_index("seq")
    c = seq % 2

    w_out_t = w_out.T
    half = w_in.shape[1] // 2
    other_in, other_out = swap(w_in), swap(w_out_t)
    par_count = swap(block_count)

    xg = pick(block_count, route_index, inputs, out_grad)
    s_own = scale(block_count, route_index, router_score[None, :])
    z_own = zdir(xg)
    xg_par = swap(xg)
    s_par = swap(s_own)
    z_par = zdir(xg_par)
    z_two = zdir(z_own)
    far_par = swap(z_own)
    far_own = swap(z_par)
    two_par = swap(z_two)
    own_rows = (xg, z_own, far_own, z_two)
    par_rows = (xg_par, z_par, far_par, two_par)

    def cut(w):
        return lax.dynamic_slice_in_dim(w, c * half, half, axis=1)

    def joined(w, other):
        a, b = cut(w), cut(other)
        return jnp.where(c == 0, jnp.concatenate([a, b], 0), jnp.concatenate([b, a], 0))

    s = jnp.stack([joined(w_in, other_in), joined(w_out_t, other_out)])
    p_f, p_b = hop(s, 1, 0), hop(s, -1, 0)
    y0f, y0b = hop(s, 1, 1), hop(s, -1, 1)
    h_in, h_out = hop(p_f[0], 1, 0), hop(p_b[1], -1, 0)
    r = jnp.concatenate([p_f[:1], p_b[:1], p_f[1:], p_b[1:]], 0)
    yrf, yrb = hop(r, 1, 1), hop(r, -1, 1)
    h = jnp.stack([h_in, h_out])
    yhf, yhb = hop(h, 1, 1), hop(h, -1, 1)
    a_in, a_out = hop(y0f[0], 1, 1), hop(y0b[1], -1, 1)
    r_in, r_out = hop(yrf[:2], 1, 1), hop(yrb[2:], -1, 1)
    low, high = yhf[0], yhb[1]
    b_in, b_out = hop(low, 1, 1), hop(high, -1, 1)

    pieces = (s, p_f, p_b, h_in, h_out, y0f, y0b, yrf, yrb, yhf, yhb)
    pieces = pieces + (a_in, r_in, b_in, a_out, r_out, b_out)
    o_par, score_par = half_stage((0, 2), par_count, par_rows, s_par, pieces)
    other = swap(o_par)
    score_other = swap(score_par)
    o_a, score_a = half_stage((0, 1), block_count, own_rows, s_own, pieces)
    o_b, score_own = half_stage((1, 2), block_count, own_rows, s_own, pieces, (score_a,))

    mid = ROWS // 2
    add_a, sent_a = merge((0, 2), 0, o_a, other)
    through_f, low_a = zhop(add_a, 1), zhop(sent_a, -1)
    add_b, sent_b = merge((0, 1), mid, o_b, other)
    through_b, low_b = zhop(add_b, -1), zhop(sent_b, 1)

    row_scores = score_own + score_other
    up_one, down_one = zhop(row_scores, 1), zhop(row_scores, -1)
    row_scores = (row_scores + zhop(row_scores, 2)) + (up_one + down_one)

    (more_a,) = merge((1,), 0, o_a, other, through_f)
    (more_b,) = merge((2,), mid, o_b, other, through_b)
    full_a, full_b = zhop(more_a, 1), zhop(more_b, -1)
    hot, score_grad = marks(block_count, route_index, row_scores)
    held = early(block_count, hot, o_a, other, full_a, low_a)
    input_grad = place(block_count, hot, held, o_b, other, full_b, low_b)
    return (input_grad, score_grad.reshape(router_score.shape))


def solution(mesh):
    placed = (
        P("seq", "tensor"),
        P("seq", "tensor"),
        P("seq"),
        P("seq", None),
        P("seq"),
        P("seq", "tensor"),
        P("tensor", "seq"),
    )
    return jax.shard_map(
        branch,
        mesh=mesh,
        in_specs=placed,
        out_specs=(P("seq", "tensor"), P("seq")),
        check_vma=False,
    )
```
